32 devices in a mesh: row: 4 (over z), col: 8 (over y, x, core).
Axes of the slice: x: 2, y: 2, z: 4, core: 2. Of those that a mesh axis runs over, the one named last changes fastest.
Arguments:
- hamiltonian: bfloat16 [2048, 2048], P('row', 'col'), may hold values from -0.3 to 0.3
- pattern: int32 [16, 16], replicated, may hold values from 0 to 1, as said below
- tile_lists: int32 [32, 8], replicated, may hold values from 0 to 15, as said below
- orders: int32 [32], replicated, may hold values from 6 to 8
- shift: float32 [1], replicated, may hold values from -0.5 to 0.5
Outputs:
- density: bfloat16 [2048, 2048], P('row', 'col')
- php: float32 [2048, 2048], P('row', 'col')
The draws below stay inside these ranges and needn't reach their ends.
Inputs may be any that keep to these rules, and one draw needn't show every extreme that they name: `pattern`: Symmetric, with zeros on the diagonal. `tile_lists`: row s begins with tile s * 64 // 128; its entries lie in distinct groups of 2 consecutive tiles, and the second lies in the group that shares a group of 4 consecutive tiles with the first. Entries from position orders[s] on are not used.
All inputs are finite; a program needn't handle non-finite values.
Results may differ from the reference program's by a relative error of at most 0.0073.
Values may be sent and summed in bfloat16 or wider, within the bound.
A program may use at most 64 MiB of HBM per device.

```python
import jax
import jax.numpy as jnp
from jax import lax

TILE = 128
TPC = 2
MAXT = 8
MINT = 6
ITERS = 3
NB = 16
NH = 2048
SUBS = 32
CW = 64


def draw_hamiltonian(key, part):
    raw = jax.random.truncated_normal(key, -4.0, 4.0, (NH, NH), jnp.float32) * 0.05
    mirrored = (raw + raw.T) * 0.5 ** 0.5
    return mirrored.astype(jnp.bfloat16)


def draw_pattern(key, part):
    picks = jax.random.randint(jax.random.fold_in(key, 5), (NB, NB), 0, 4, dtype=jnp.int32)
    upper = jnp.triu((picks == 0).astype(jnp.int32), 1)
    return (upper + upper.T).astype(jnp.int32)


def one_list(key, index):
    groups = NB // TPC
    center = index * CW // TILE
    home = center // TPC
    partner = jnp.bitwise_xor(home, 1)
    scores = jax.random.permutation(jax.random.fold_in(key, 7), groups).astype(jnp.int32)
    positions = jnp.arange(groups, dtype=jnp.int32)
    scores = jnp.where(positions == home, -2, scores)
    scores = jnp.where(positions == partner, -1, scores)
    chosen = jnp.argsort(scores, stable=True)[:MAXT].astype(jnp.int32)
    offsets = jax.random.randint(jax.random.fold_in(key, 11), (MAXT,), 0, TPC, dtype=jnp.int32)
    tiles = chosen * TPC + offsets
    return tiles.at[0].set(center.astype(jnp.int32))


def draw_tile_lists(key, part):
    keys = jax.random.split(jax.random.fold_in(key, 3), SUBS)
    return jax.vmap(one_list)(keys, jnp.arange(SUBS, dtype=jnp.int32)).astype(jnp.int32)


def with_ends(values, rng, smallest, top_value):
    longest = values.shape.index(max(values.shape))
    spots = []
    for shift in (0, 1):
        where = [jax.random.randint(jax.random.fold_in(rng, axis), (), 0, length) for axis, length in enumerate(values.shape)]
        where[longest] = (where[longest] + shift) % values.shape[longest]
        spots.append(tuple(where))
    return values.at[spots[0]].set(smallest).at[spots[1]].set(top_value)


def setup_inputs(seed: int = 0) -> dict:
    key_of = jax.random.split(jax.random.key(seed), 6)
    hamiltonian = draw_hamiltonian(jax.random.fold_in(key_of[5], 71), 0)
    pattern = draw_pattern(jax.random.fold_in(key_of[5], 71), 0)
    tile_lists = draw_tile_lists(jax.random.fold_in(key_of[5], 71), 0)
    orders = with_ends(jax.random.randint(key_of[3], (SUBS,), MINT, MAXT + 1), jax.random.fold_in(key_of[3], 1), MINT, MAXT).astype(jnp.int32)
    shift = jnp.clip(jax.random.uniform(key_of[4], (1,), jnp.float32, -0.5, 0.5), -0.5, 0.5)
    return {"hamiltonian": hamiltonian, "pattern": pattern, "tile_lists": tile_lists, "orders": orders, "shift": shift}


def masked_blocks(hamiltonian, pattern):
    count = pattern.shape[0]
    keep = jnp.maximum(pattern, jnp.eye(count, dtype=jnp.int32))
    blocks = hamiltonian.reshape(count, TILE, count, TILE).transpose(0, 2, 1, 3)
    return jnp.where(keep[:, :, None, None] > 0, blocks, jnp.zeros_like(blocks))

def newton_density(sub, live_rows, potential):
    eye = jnp.eye(sub.shape[0], dtype=jnp.float32)
    shifted = sub.astype(jnp.float32) - potential * eye * live_rows[None, :]
    row_squares = lax.optimization_barrier(jnp.sum(shifted * shifted, axis=1))
    scale = jnp.abs(potential) + 2.0 * jnp.sqrt(jnp.max(row_squares) + 1e-06)
    iterate = (shifted / scale).astype(jnp.bfloat16)
    product = shifted
    for step in range(ITERS):
        square = jnp.dot(iterate, iterate, preferred_element_type=jnp.float32)
        factor = (1.5 * eye - 0.5 * square).astype(jnp.bfloat16)
        product = jnp.dot(iterate, factor, preferred_element_type=jnp.float32)
        if step + 1 < ITERS:
            iterate = product.astype(jnp.bfloat16)
    return 0.5 * (eye - product)

def reference(hamiltonian, pattern, tile_lists, orders, shift):
    count = pattern.shape[0]
    blocks = masked_blocks(hamiltonian, pattern)
    potential = shift[0]
    total = tile_lists.shape[0]
    width = count * TILE // total

    def solve(index):
        tiles = tile_lists[index]
        live = jnp.arange(MAXT, dtype=jnp.int32) < orders[index]
        sub = jnp.take(jnp.take(blocks, tiles, axis=0), tiles, axis=1)
        both = live[:, None] & live[None, :]
        sub = jnp.where(both[:, :, None, None], sub, jnp.zeros_like(sub))
        sub = sub.transpose(0, 2, 1, 3).reshape(MAXT * TILE, MAXT * TILE)
        live_rows = jnp.repeat(live.astype(jnp.float32), TILE)
        dens = newton_density(sub, live_rows, potential)
        offset = (index * width % TILE).astype(jnp.int32)
        central = lax.dynamic_slice_in_dim(dens, offset, width, 1).astype(jnp.bfloat16)
        central = central.astype(jnp.float32).reshape(MAXT, TILE, width)
        chooser = ((tiles[:, None] == jnp.arange(count, dtype=jnp.int32)[None, :]) & live[:, None]).astype(jnp.float32)
        placed = jnp.einsum('ia,itw->atw', chooser, central)
        return placed.astype(jnp.bfloat16)
    pieces = lax.map(solve, jnp.arange(total, dtype=jnp.int32))
    density = pieces.transpose(1, 2, 0, 3).reshape(count * TILE, total * width)
    ham = blocks.transpose(0, 2, 1, 3).reshape(count * TILE, count * TILE)
    hp = jnp.dot(ham, density, preferred_element_type=jnp.float32).astype(jnp.bfloat16)
    php = jnp.dot(density, hp, preferred_element_type=jnp.float32)
    return (density, php)
```

```python
import functools

import jax
import jax.numpy as jnp
from jax import lax
from jax.experimental import pallas as pl
from jax.experimental.pallas import tpu as pltpu
from jax.sharding import PartitionSpec as P

TILE = 128
TPC = 2
MAXT = 8
ITERS = 3
BF = jnp.bfloat16
F32 = jnp.float32
MESH = pl.DeviceIdType.MESH
SPAN = MAXT * TILE
BLOCK = 256


def eye_block(rows, cols, shift):
    r = lax.broadcasted_iota(jnp.int32, (rows, cols), 0)
    c = lax.broadcasted_iota(jnp.int32, (rows, cols), 1)
    return r == c + shift


def kernel(
    rows_n, cols_n, code, lists, orders, pattern, shift, ham,
    dens_out, php_out,
    strip, stage, arr, xa, fb, turned, cent, call, pall, pt, ptc, gall, ht, acc,
    up_s, up_r, dn_s, dn_r, aa_s, aa_r, cz_s, cz_r, pa_s, pa_r, pf_s, pf_r, ga_s, ga_r, gf_s, gf_r,
):
    me_row = lax.axis_index("row")
    me_col = lax.axis_index("col")
    high, wide = ham.shape
    row_tiles = high // TILE
    gpr = row_tiles // TPC
    groups = rows_n * gpr
    width = wide // rows_n
    pairs_n = cols_n // 2
    my_pair = me_col // 2
    parity = lax.rem(me_col, 2)
    partner = my_pair * 2 + 1 - parity
    solver = me_col * rows_n + me_row

    def send(src, dst, ss, rs, row, col):
        return pltpu.make_async_remote_copy(
            src_ref=src, dst_ref=dst, send_sem=ss, recv_sem=rs,
            device_id=(row, col), device_id_type=MESH,
        )

    barrier = pltpu.get_barrier_semaphore()
    for d in range(1, rows_n):
        pl.semaphore_signal(
            barrier, inc=1, device_id=(lax.rem(me_row + d, rows_n), me_col), device_id_type=MESH)
    for d in range(1, cols_n):
        pl.semaphore_signal(
            barrier, inc=1, device_id=(me_row, lax.rem(me_col + d, cols_n)), device_id_type=MESH)
    pl.semaphore_wait(barrier, rows_n - 1 + cols_n - 1)

    def up_copy(d):
        q = me_row - d
        src = ham if d == 0 else strip.at[jnp.maximum(q, 0)]
        return send(src, strip.at[jnp.maximum(q, 0)], up_s.at[d], up_r.at[d],
                    jnp.minimum(me_row + 1, rows_n - 1), me_col)

    def dn_copy(d):
        q = me_row + d
        src = ham if d == 0 else strip.at[jnp.minimum(q, rows_n - 1)]
        return send(src, strip.at[jnp.minimum(q, rows_n - 1)], dn_s.at[d], dn_r.at[d],
                    jnp.maximum(me_row - 1, 0), me_col)

    def sends_up(d):
        return (me_row - d >= 0) & (me_row + 1 < rows_n)

    def sends_dn(d):
        return (me_row + d < rows_n) & (me_row >= 1)

    def pick(s, g):
        return lax.rem(jnp.maximum(code[s, g], 0), 2)

    def distribute(block, q):
        def one(d, carry):
            p = lax.rem(me_col + d, cols_n)
            s = p * rows_n + me_row
            right = pick(s, me_col) == 1
            for k in range(gpr):
                g = q * gpr + k
                low = pick(s, g) == 1
                base = k * TPC * TILE
                t00 = block[base:base + TILE, 0:TILE]
                t01 = block[base:base + TILE, TILE:2 * TILE]
                t10 = block[base + TILE:base + 2 * TILE, 0:TILE]
                t11 = block[base + TILE:base + 2 * TILE, TILE:2 * TILE]
                top = jnp.where(right, t01, t00)
                bottom = jnp.where(right, t11, t10)
                stage[p, g] = jnp.where(low, bottom, top)

            @pl.when(d > 0)
            def _():
                send(stage.at[p, pl.ds(q * gpr, gpr)], arr.at[me_col, pl.ds(q * gpr, gpr)],
                     aa_s.at[q, p], aa_r.at[q, me_col], me_row, p).start()

            @pl.when(d == 0)
            def _():
                for k in range(gpr):
                    arr[me_col, q * gpr + k] = stage[me_col, q * gpr + k]
            return carry
        lax.fori_loop(0, cols_n, one, 0)

    def turn(block, q):
        for a in range(row_tiles):
            for b in range(TPC):
                ga = q * row_tiles + a
                gb = me_col * TPC + b
                keep = (pattern[ga, gb] == 1) | (ga == gb)
                t = block[a * TILE:(a + 1) * TILE, b * TILE:(b + 1) * TILE]
                t = jnp.where(keep, t, jnp.zeros_like(t))
                ht[q * gpr + a // TPC, b * TILE:(b + 1) * TILE,
                   (a % TPC) * TILE:(a % TPC + 1) * TILE] = t.T

    @pl.when(sends_up(0))
    def _():
        up_copy(0).start()

    @pl.when(sends_dn(0))
    def _():
        dn_copy(0).start()

    distribute(ham, me_row)
    for d in range(rows_n - 1):
        @pl.when(me_row - 1 - d >= 0)
        def _():
            up_copy(d).wait_recv()

            @pl.when(sends_up(d + 1))
            def _():
                up_copy(d + 1).start()
            distribute(strip.at[jnp.maximum(me_row - 1 - d, 0)], jnp.maximum(me_row - 1 - d, 0))

        @pl.when(me_row + 1 + d < rows_n)
        def _():
            dn_copy(d).wait_recv()

            @pl.when(sends_dn(d + 1))
            def _():
                dn_copy(d + 1).start()
            q = jnp.minimum(me_row + 1 + d, rows_n - 1)
            distribute(strip.at[q], q)

    turn(ham, me_row)

    def turn_other(d, carry):
        q = lax.rem(me_row + d, rows_n)
        turn(strip.at[q], q)
        return carry
    lax.fori_loop(1, rows_n, turn_other, 0)

    def wait_all(d, carry):
        p = lax.rem(me_col + d, cols_n)

        def inner(q, c):
            send(stage.at[p, pl.ds(q * gpr, gpr)], arr.at[p, pl.ds(q * gpr, gpr)],
                 aa_s.at[q, p], aa_r.at[q, p], me_row, p).wait()
            return c
        return lax.fori_loop(0, rows_n, inner, carry)
    lax.fori_loop(1, cols_n, wait_all, 0)

    potential = shift[0]
    order = orders[solver]
    eye = eye_block(TILE, TILE, 0)
    biggest = jnp.zeros((TILE, 1), F32)

    def build(i, most):
        ti = lists[solver, i]
        sums = jnp.zeros((TILE, TILE), F32)
        for j in range(MAXT):
            tj = lists[solver, j]
            keep = (i < order) & (j < order) & ((pattern[ti, tj] == 1) | (i == j))
            t = arr[tj // TPC, ti // TPC]
            t = jnp.where(keep, t, jnp.zeros_like(t))
            xa[pl.ds(pl.multiple_of(i * TILE, TILE), TILE), j * TILE:(j + 1) * TILE] = t
            v = t.astype(F32)
            move = jnp.where((i == j) & (i < order), potential, 0.0)
            v = v - jnp.where(eye, move, 0.0)
            sums += v * v
        return jnp.maximum(most, jnp.sum(sums, axis=1, keepdims=True))
    biggest = lax.fori_loop(0, MAXT, build, biggest)
    top = jnp.max(biggest, axis=0, keepdims=True)
    scale = jnp.abs(potential) + 2.0 * jnp.sqrt(top + 1e-06)
    inverse = 1.0 / scale

    def norm(i, carry):
        rows = pl.ds(pl.multiple_of(i * TILE, TILE), TILE)
        v = xa[rows, :].astype(F32)
        hit = eye_block(TILE, SPAN, 0 - i * TILE)
        move = jnp.where(i < order, potential, 0.0)
        v = v - jnp.where(hit, move, 0.0)
        xa[rows, :] = (v * inverse).astype(BF)
        return carry
    lax.fori_loop(0, MAXT, norm, 0)

    x, f = xa, fb
    for step in range(ITERS - 1):
        y = turned

        def square(n, carry):
            cols = pl.ds(pl.multiple_of(n * BLOCK, BLOCK), BLOCK)
            q = jnp.dot(x[...], x[:, cols], preferred_element_type=F32)
            hit = eye_block(SPAN, BLOCK, n * BLOCK)
            f[:, cols] = (jnp.where(hit, 1.5, 0.0) - 0.5 * q).astype(BF)
            return carry
        lax.fori_loop(0, SPAN // BLOCK, square, 0)

        def times(n, carry):
            cols = pl.ds(pl.multiple_of(n * BLOCK, BLOCK), BLOCK)
            y[:, cols] = jnp.dot(x[...], f[:, cols], preferred_element_type=F32).astype(BF)
            return carry
        lax.fori_loop(0, SPAN // BLOCK, times, 0)
        x, turned = y, x
    q = jnp.dot(x[...], x[:, 0:TILE], preferred_element_type=F32)
    hit = eye_block(SPAN, TILE, 0)
    f[:, 0:TILE] = (jnp.where(hit, 1.5, 0.0) - 0.5 * q).astype(BF)
    y3 = jnp.dot(x[...], f[:, 0:TILE], preferred_element_type=F32)
    dens = (0.5 * (jnp.where(hit, 1.0, 0.0) - y3)).astype(BF)
    for i in range(MAXT):
        cent[i] = dens[i * TILE:(i + 1) * TILE, :].T

    offset = pl.multiple_of(lax.rem(solver * width, TILE), width)
    my_rows = pl.ds(pl.multiple_of(me_row * width, width), width)

    def place(g, carry):
        where = code[solver, g]
        t = cent[jnp.maximum(where, 0) // 2, pl.ds(offset, width), :]
        call[g, my_rows, :] = jnp.where(where >= 0, t, jnp.zeros_like(t))
        return carry
    lax.fori_loop(0, groups, place, 0)

    def cz_copy(e, d):
        to = lax.rem(me_row + d, rows_n)
        part = lax.rem(me_row + d + e, rows_n)
        part_ref = call.at[pl.ds(part * gpr, gpr), my_rows, :]
        return send(part_ref, part_ref, cz_s.at[e, d], cz_r.at[e, d], to, me_col)

    for e in range(rows_n):
        for d in range(1, rows_n):
            cz_copy(e, d).start()
    for d in range(1, rows_n):
        cz_copy(0, d).wait_recv()

    mine = call.at[pl.ds(me_row * gpr, gpr)]

    def gather(src, buf, s1, r1, s2, r2):
        for d in range(1, pairs_n):
            p = lax.rem(my_pair + d, pairs_n) * 2 + parity
            send(src, buf.at[me_col], s1.at[d], r1.at[d], me_row, p).start()
        send(src, buf.at[me_col], s2.at[0], r2.at[0], me_row, partner).start()

    def arrive(buf, s1, r1, s2, r2, d):
        p = lax.rem(my_pair + pairs_n - d, pairs_n) * 2 + parity
        ref = buf.at[p]
        send(ref, ref, s1.at[d], r1.at[d], me_row, p).wait_recv()
        send(ref, ref, s2.at[d], r2.at[d], me_row, partner).start()
        return p

    def arrive2(buf, s2, r2, d):
        p = lax.rem(my_pair + pairs_n - d, pairs_n) * 2 + (1 - parity)
        ref = buf.at[p]
        send(ref, ref, s2.at[d], r2.at[d], me_row, partner).wait_recv()
        return p

    def drain(src, buf, s1, r1, s2, r2):
        for d in range(pairs_n):
            if d:
                send(src, buf.at[me_col], s1.at[d], r1.at[d], me_row, partner).wait_send()
            send(src, buf.at[me_col], s2.at[d], r2.at[d], me_row, partner).wait_send()

    gather(mine, pall, pa_s, pa_r, pf_s, pf_r)

    def spread(src, c):
        for q in range(rows_n):
            s = c * rows_n + q
            for t in range(row_tiles):
                cd = code[s, me_row * gpr + t // TPC]
                v = src[t // TPC, q * width:(q + 1) * width, :]
                ok = (cd >= 0) & (lax.rem(jnp.maximum(cd, 0), 2) == t % TPC)
                pt[q * width:(q + 1) * width, t * TILE:(t + 1) * TILE] = jnp.where(
                    ok, v, jnp.zeros_like(v))

    def term(src, c, first=False):
        spread(src, c)
        v = jnp.dot(ht[c], pt[...], preferred_element_type=F32)
        if first:
            acc[...] = v
        else:
            acc[...] += v

    term(mine, me_col, True)
    dens_out[...] = pt[...].T
    for d in range(1, pairs_n):
        p = arrive(pall, pa_s, pa_r, pf_s, pf_r, d)
        term(pall.at[p], p)
    for d in range(pairs_n):
        p = arrive2(pall, pf_s, pf_r, d)
        term(pall.at[p], p)
    gall[me_col] = acc[...].astype(BF)
    own = gall.at[me_col]
    gather(own, gall, ga_s, ga_r, gf_s, gf_r)

    for e in range(1, rows_n):
        for d in range(1, rows_n):
            cz_copy(e, d).wait_recv()
    for q in range(rows_n):
        s = me_col * rows_n + q
        for g in range(groups):
            cd = code[s, g]
            v = call[g, q * width:(q + 1) * width, :]
            for h in range(TPC):
                ok = (cd >= 0) & (lax.rem(jnp.maximum(cd, 0), 2) == h)
                ptc[g, q * width:(q + 1) * width,
                    h * TILE:(h + 1) * TILE] = jnp.where(ok, v, jnp.zeros_like(v))

    acc[...] = jnp.dot(ptc[me_col], own[...], preferred_element_type=F32)
    for d in range(1, pairs_n):
        p = arrive(gall, ga_s, ga_r, gf_s, gf_r, d)
        acc[...] += jnp.dot(ptc[p], gall[p], preferred_element_type=F32)
    for d in range(pairs_n):
        p = arrive2(gall, gf_s, gf_r, d)
        acc[...] += jnp.dot(ptc[p], gall[p], preferred_element_type=F32)
    php_out[...] = acc[...].T

    drain(mine, pall, pa_s, pa_r, pf_s, pf_r)
    drain(own, gall, ga_s, ga_r, gf_s, gf_r)
    for e in range(rows_n):
        for d in range(1, rows_n):
            cz_copy(e, d).wait_send()
    for d in range(rows_n):
        @pl.when(sends_up(d))
        def _():
            up_copy(d).wait_send()

        @pl.when(sends_dn(d))
        def _():
            dn_copy(d).wait_send()


def per_device(hamiltonian, pattern, tile_lists, orders, shift):
    rows_n = lax.axis_size("row")
    cols_n = lax.axis_size("col")
    high, wide = hamiltonian.shape
    groups = pattern.shape[0] // TPC
    gpr = high // TILE // TPC
    width = wide // rows_n
    pairs_n = cols_n // 2
    steps = jnp.arange(MAXT, dtype=jnp.int32)
    g = jnp.arange(groups, dtype=jnp.int32)
    hit = (tile_lists[:, None, :] // TPC == g[None, :, None]) & (
        steps[None, None, :] < orders[:, None, None])
    code = jnp.max(
        jnp.where(hit, steps[None, None, :] * TPC + tile_lists[:, None, :] % TPC, -1), axis=2)
    dma = pltpu.SemaphoreType.DMA
    smem = pl.BlockSpec(memory_space=pltpu.SMEM)
    vmem = pl.BlockSpec(memory_space=pltpu.VMEM)
    return pl.pallas_call(
        functools.partial(kernel, rows_n, cols_n),
        out_shape=(
            jax.ShapeDtypeStruct((high, wide), BF),
            jax.ShapeDtypeStruct((high, wide), F32),
        ),
        in_specs=[smem] * 5 + [vmem],
        out_specs=(vmem, vmem),
        scratch_shapes=[
            pltpu.VMEM((rows_n, high, wide), BF),
            pltpu.VMEM((cols_n, groups, TILE, TILE), BF),
            pltpu.VMEM((cols_n, groups, TILE, TILE), BF),
            pltpu.VMEM((SPAN, SPAN), BF),
            pltpu.VMEM((SPAN, SPAN), BF),
            pltpu.VMEM((SPAN, SPAN), BF),
            pltpu.VMEM((MAXT, TILE, TILE), BF),
            pltpu.VMEM((groups, wide, TILE), BF),
            pltpu.VMEM((cols_n, gpr, wide, TILE), BF),
            pltpu.VMEM((wide, high), BF),
            pltpu.VMEM((groups, wide, TPC * TILE), BF),
            pltpu.VMEM((cols_n, wide, high), BF),
            pltpu.VMEM((groups, wide, TPC * TILE), BF),
            pltpu.VMEM((wide, high), F32),
            dma((rows_n,)), dma((rows_n,)), dma((rows_n,)), dma((rows_n,)),
            dma((rows_n, cols_n)), dma((rows_n, cols_n)),
            dma((rows_n, rows_n)), dma((rows_n, rows_n)),
            dma((pairs_n,)), dma((pairs_n,)), dma((pairs_n,)), dma((pairs_n,)),
            dma((pairs_n,)), dma((pairs_n,)), dma((pairs_n,)), dma((pairs_n,)),
        ],
        compiler_params=pltpu.CompilerParams(
            collective_id=0, has_side_effects=True, vmem_limit_bytes=60000000),
    )(code, tile_lists, orders, pattern, shift, hamiltonian)


def solution(mesh):
    in_specs = (P("row", "col"), P(), P(), P(), P())
    out_specs = (P("row", "col"), P("row", "col"))
    return jax.shard_map(
        per_device, mesh=mesh, in_specs=in_specs, out_specs=out_specs, check_vma=False
    )
```

```python
import functools

import jax
import jax.numpy as jnp
from jax import lax
from jax.experimental import pallas as pl
from jax.experimental.pallas import tpu as pltpu
from jax.sharding import PartitionSpec as P

TILE = 128
TPC = 2
MAXT = 8
ITERS = 3
BF = jnp.bfloat16
F32 = jnp.float32
MESH = pl.DeviceIdType.MESH
SPAN = MAXT * TILE
BLOCK = 256


def eye_block(rows, cols, shift):
    r = lax.broadcasted_iota(jnp.int32, (rows, cols), 0)
    c = lax.broadcasted_iota(jnp.int32, (rows, cols), 1)
    return r == c + shift


def kernel(
    rows_n, cols_n, code, lists, orders, pattern, shift, ham,
    dens_out, php_out,
    strip, stage, arr, xa, fb, turned, cent, call, pall, pt, ptc, gall, ht, acc,
    up_s, up_r, dn_s, dn_r, uq_s, uq_r, dq_s, dq_r, bz_s, bz_r, aa_s, aa_r, cz_s, cz_r, pa_s, pa_r, pf_s, pf_r, ga_s, ga_r, gf_s, gf_r,
):
    me_row = lax.axis_index("row")
    me_col = lax.axis_index("col")
    high, wide = ham.shape
    row_tiles = high // TILE
    gpr = row_tiles // TPC
    groups = rows_n * gpr
    width = wide // rows_n
    pairs_n = cols_n // 2
    my_pair = me_col // 2
    parity = lax.rem(me_col, 2)
    partner = my_pair * 2 + 1 - parity
    solver = me_col * rows_n + me_row

    def send(src, dst, ss, rs, row, col):
        return pltpu.make_async_remote_copy(
            src_ref=src, dst_ref=dst, send_sem=ss, recv_sem=rs,
            device_id=(row, col), device_id_type=MESH,
        )

    barrier = pltpu.get_barrier_semaphore()
    for d in range(1, rows_n):
        pl.semaphore_signal(
            barrier, inc=1, device_id=(lax.rem(me_row + d, rows_n), me_col), device_id_type=MESH)
    for d in range(1, cols_n):
        pl.semaphore_signal(
            barrier, inc=1, device_id=(me_row, lax.rem(me_col + d, cols_n)), device_id_type=MESH)
    pl.semaphore_wait(barrier, rows_n - 1 + cols_n - 1)

    half_rows = TPC * TILE

    def first(q):
        return jnp.where(q == my_pair, 0, jnp.where(q < my_pair, parity, 1 - parity))

    def rows_of(half):
        return pl.ds(pl.multiple_of(half * half_rows, half_rows), half_rows)

    def chain(d, up, other):
        q = jnp.clip(me_row - d if up else me_row + d, 0, rows_n - 1)
        to = jnp.clip(me_row + 1 if up else me_row - 1, 0, rows_n - 1)
        half = 1 - first(q) if other else first(q)
        rows = rows_of(half)
        src = ham.at[rows] if d == 0 else strip.at[q, rows]
        ss, rs = ((uq_s, uq_r) if up else (dq_s, dq_r)) if other else (
            (up_s, up_r) if up else (dn_s, dn_r))
        return send(src, strip.at[q, rows], ss.at[d], rs.at[d], to, me_col)

    def source(d, up):
        return me_row - d if up else me_row + d

    def sends(d, up):
        q = source(d, up)
        return (q >= 0) & (me_row + 1 < rows_n) if up else (q < rows_n) & (me_row >= 1)

    def start_chain(d, up):
        @pl.when(sends(d, up))
        def _():
            chain(d, up, False).start()

        @pl.when(sends(d, up) & (source(d, up) == my_pair))
        def _():
            chain(d, up, True).start()

    def rest(d):
        rows = rows_of(1 - first(me_row))
        return send(ham.at[rows], strip.at[me_row, rows], bz_s.at[d], bz_r.at[d],
                    lax.rem(me_row + d, rows_n), me_col)

    def rest_in(d):
        q = lax.rem(me_row + rows_n - d, rows_n)
        ref = strip.at[q, rows_of(1 - first(q))]
        return q, send(ref, ref, bz_s.at[d], bz_r.at[d], lax.rem(me_row + d, rows_n), me_col)

    def pick(s, g):
        return lax.rem(jnp.maximum(code[s, g], 0), 2)

    def distribute(block, q, half, slot):
        g = q * gpr + half
        base = half * half_rows

        def one(d, carry):
            p = lax.rem(me_col + d, cols_n)
            s = p * rows_n + me_row
            right = pick(s, me_col) == 1
            low = pick(s, g) == 1
            above = pl.ds(pl.multiple_of(base, TILE), TILE)
            below = pl.ds(pl.multiple_of(base + TILE, TILE), TILE)
            top = jnp.where(right, block[above, TILE:2 * TILE], block[above, 0:TILE])
            bottom = jnp.where(right, block[below, TILE:2 * TILE], block[below, 0:TILE])
            tile = jnp.where(low, bottom, top)

            @pl.when(d > 0)
            def _():
                stage[p, slot] = tile
                send(stage.at[p, slot], arr.at[me_col, slot],
                     aa_s.at[slot, p], aa_r.at[slot, me_col], me_row, p).start()

            @pl.when(d == 0)
            def _():
                arr[me_col, slot] = tile
            return carry
        lax.fori_loop(0, cols_n, one, 0)

    def deal(block, q):
        distribute(block, q, first(q), q)

        @pl.when(q == my_pair)
        def _():
            distribute(block, q, 1 - first(q), rows_n)

    def turn(block, q, half):
        for a in range(TPC):
            for b in range(TPC):
                ga = q * row_tiles + half * TPC + a
                gb = me_col * TPC + b
                keep = (pattern[ga, gb] == 1) | (ga == gb)
                rows = pl.ds(pl.multiple_of(half * half_rows + a * TILE, TILE), TILE)
                t = block[rows, b * TILE:(b + 1) * TILE]
                t = jnp.where(keep, t, jnp.zeros_like(t))
                ht[q * gpr + half, b * TILE:(b + 1) * TILE, a * TILE:(a + 1) * TILE] = t.T

    start_chain(0, True)
    start_chain(0, False)
    deal(ham, me_row)
    for d in range(rows_n - 1):
        for up in (True, False):
            q = source(d + 1, up)
            here = (q >= 0) & (q < rows_n)

            @pl.when(here)
            def _():
                chain(d, up, False).wait_recv()

            @pl.when(here & (q == my_pair))
            def _():
                chain(d, up, True).wait_recv()

            @pl.when(here)
            def _():
                start_chain(d + 1, up)
                at = jnp.clip(q, 0, rows_n - 1)
                deal(strip.at[at], at)

    @pl.when(me_row != my_pair)
    def _():
        for d in range(1, rows_n):
            rest(d).start()

    turn(ham, me_row, 0)
    turn(ham, me_row, 1)

    def turn_other(d, carry):
        q = lax.rem(me_row + d, rows_n)
        turn(strip.at[q], q, first(q))
        return carry
    lax.fori_loop(1, rows_n, turn_other, 0)

    def wait_all(d, carry):
        p = lax.rem(me_col + d, cols_n)

        def inner(slot, c):
            send(stage.at[p, slot], arr.at[p, slot],
                 aa_s.at[slot, p], aa_r.at[slot, p], me_row, p).wait()
            return c
        return lax.fori_loop(0, rows_n + 1, inner, carry)
    lax.fori_loop(1, cols_n, wait_all, 0)

    potential = shift[0]
    order = orders[solver]

    def slot_of(g, h):
        return jnp.where((g // TPC == h // TPC) & (lax.rem(g, TPC) == 1), rows_n, g // TPC)

    for i in range(MAXT):
        ti = lists[solver, i]
        gi = ti // TPC
        for j in range(i, MAXT):
            tj = lists[solver, j]
            gj = tj // TPC
            keep = (i < order) & (j < order)
            here = slice(i * TILE, (i + 1) * TILE)
            there = slice(j * TILE, (j + 1) * TILE)
            if i == j:
                t = arr[gi, slot_of(gi, gi)]
                xa[here, here] = jnp.where(keep, t, jnp.zeros_like(t))
                continue
            keep = keep & (pattern[ti, tj] == 1)
            even = lax.rem(gi + gj, 2) == 0
            ri, rj = gi // TPC, gj // TPC
            as_is = (ri == rj) | ((ri < rj) & even) | ((ri > rj) & jnp.logical_not(even))
            w = jnp.where(as_is, arr[gj, slot_of(gi, gj)], arr[gi, slot_of(gj, gi)])
            w = jnp.where(keep, w, jnp.zeros_like(w))
            wt = w.T
            xa[here, there] = jnp.where(as_is, w, wt)
            xa[there, here] = jnp.where(as_is, wt, w)

    def squares(i, most):
        v = xa[pl.ds(pl.multiple_of(i * TILE, TILE), TILE), :].astype(F32)
        move = jnp.where(i < order, potential, 0.0)
        v = v - jnp.where(eye_block(TILE, SPAN, 0 - i * TILE), move, 0.0)
        return jnp.maximum(most, jnp.sum(v * v, axis=1, keepdims=True))
    biggest = lax.fori_loop(0, MAXT, squares, jnp.zeros((TILE, 1), F32))
    top = jnp.max(biggest, axis=0, keepdims=True)
    scale = jnp.abs(potential) + 2.0 * jnp.sqrt(top + 1e-06)
    inverse = 1.0 / scale

    def norm(i, carry):
        rows = pl.ds(pl.multiple_of(i * TILE, TILE), TILE)
        v = xa[rows, :].astype(F32)
        hit = eye_block(TILE, SPAN, 0 - i * TILE)
        move = jnp.where(i < order, potential, 0.0)
        v = v - jnp.where(hit, move, 0.0)
        xa[rows, :] = (v * inverse).astype(BF)
        return carry
    lax.fori_loop(0, MAXT, norm, 0)

    x, f = xa, fb
    for step in range(ITERS - 1):
        y = turned

        def square(n, carry):
            cols = pl.ds(pl.multiple_of(n * BLOCK, BLOCK), BLOCK)
            q = jnp.dot(x[...], x[:, cols], preferred_element_type=F32)
            hit = eye_block(SPAN, BLOCK, n * BLOCK)
            f[:, cols] = (jnp.where(hit, 1.5, 0.0) - 0.5 * q).astype(BF)
            return carry
        lax.fori_loop(0, SPAN // BLOCK, square, 0)

        def times(n, carry):
            cols = pl.ds(pl.multiple_of(n * BLOCK, BLOCK), BLOCK)
            y[:, cols] = jnp.dot(x[...], f[:, cols], preferred_element_type=F32).astype(BF)
            return carry
        lax.fori_loop(0, SPAN // BLOCK, times, 0)
        x, turned = y, x
    q = jnp.dot(x[...], x[:, 0:TILE], preferred_element_type=F32)
    hit = eye_block(SPAN, TILE, 0)
    f[:, 0:TILE] = (jnp.where(hit, 1.5, 0.0) - 0.5 * q).astype(BF)
    y3 = jnp.dot(x[...], f[:, 0:TILE], preferred_element_type=F32)
    dens = (0.5 * (jnp.where(hit, 1.0, 0.0) - y3)).astype(BF)
    for i in range(MAXT):
        cent[i] = dens[i * TILE:(i + 1) * TILE, :].T

    offset = pl.multiple_of(lax.rem(solver * width, TILE), width)
    my_rows = pl.ds(pl.multiple_of(me_row * width, width), width)

    def place(g, carry):
        where = code[solver, g]
        t = cent[jnp.maximum(where, 0) // 2, pl.ds(offset, width), :]
        call[g, my_rows, :] = jnp.where(where >= 0, t, jnp.zeros_like(t))
        return carry
    lax.fori_loop(0, groups, place, 0)

    def cz_copy(e, d):
        to = lax.rem(me_row + d, rows_n)
        part = lax.rem(me_row + d + e, rows_n)
        part_ref = call.at[pl.ds(part * gpr, gpr), my_rows, :]
        return send(part_ref, part_ref, cz_s.at[e, d], cz_r.at[e, d], to, me_col)

    for e in range(rows_n):
        for d in range(1, rows_n):
            cz_copy(e, d).start()

    def turn_rest(d):
        q, copy = rest_in(d)

        @pl.when(q != my_pair)
        def _():
            copy.wait_recv()
        turn(strip.at[q], q, 1 - first(q))
    for d in range(1, rows_n):
        turn_rest(d)
    for d in range(1, rows_n):
        cz_copy(0, d).wait_recv()

    mine = call.at[pl.ds(me_row * gpr, gpr)]

    def gather(src, buf, s1, r1, s2, r2):
        for d in range(1, pairs_n):
            p = lax.rem(my_pair + d, pairs_n) * 2 + parity
            send(src, buf.at[me_col], s1.at[d], r1.at[d], me_row, p).start()
        send(src, buf.at[me_col], s2.at[0], r2.at[0], me_row, partner).start()

    def arrive(buf, s1, r1, s2, r2, d):
        p = lax.rem(my_pair + pairs_n - d, pairs_n) * 2 + parity
        ref = buf.at[p]
        send(ref, ref, s1.at[d], r1.at[d], me_row, p).wait_recv()
        send(ref, ref, s2.at[d], r2.at[d], me_row, partner).start()
        return p

    def arrive2(buf, s2, r2, d):
        p = lax.rem(my_pair + pairs_n - d, pairs_n) * 2 + (1 - parity)
        ref = buf.at[p]
        send(ref, ref, s2.at[d], r2.at[d], me_row, partner).wait_recv()
        return p

    def drain(src, buf, s1, r1, s2, r2):
        for d in range(pairs_n):
            if d:
                send(src, buf.at[me_col], s1.at[d], r1.at[d], me_row, partner).wait_send()
            send(src, buf.at[me_col], s2.at[d], r2.at[d], me_row, partner).wait_send()

    gather(mine, pall, pa_s, pa_r, pf_s, pf_r)

    def spread(src, c):
        for q in range(rows_n):
            s = c * rows_n + q
            for t in range(row_tiles):
                cd = code[s, me_row * gpr + t // TPC]
                v = src[t // TPC, q * width:(q + 1) * width, :]
                ok = (cd >= 0) & (lax.rem(jnp.maximum(cd, 0), 2) == t % TPC)
                pt[q * width:(q + 1) * width, t * TILE:(t + 1) * TILE] = jnp.where(
                    ok, v, jnp.zeros_like(v))

    def term(src, c, first=False):
        spread(src, c)
        v = jnp.dot(ht[c], pt[...], preferred_element_type=F32)
        if first:
            acc[...] = v
        else:
            acc[...] += v

    term(mine, me_col, True)
    dens_out[...] = pt[...].T
    for d in range(1, pairs_n):
        p = arrive(pall, pa_s, pa_r, pf_s, pf_r, d)
        term(pall.at[p], p)
    for d in range(pairs_n):
        p = arrive2(pall, pf_s, pf_r, d)
        term(pall.at[p], p)
    gall[me_col] = acc[...].astype(BF)
    own = gall.at[me_col]
    gather(own, gall, ga_s, ga_r, gf_s, gf_r)

    for e in range(1, rows_n):
        for d in range(1, rows_n):
            cz_copy(e, d).wait_recv()
    for q in range(rows_n):
        s = me_col * rows_n + q
        for g in range(groups):
            cd = code[s, g]
            v = call[g, q * width:(q + 1) * width, :]
            for h in range(TPC):
                ok = (cd >= 0) & (lax.rem(jnp.maximum(cd, 0), 2) == h)
                ptc[g, q * width:(q + 1) * width,
                    h * TILE:(h + 1) * TILE] = jnp.where(ok, v, jnp.zeros_like(v))

    acc[...] = jnp.dot(ptc[me_col], own[...], preferred_element_type=F32)
    for d in range(1, pairs_n):
        p = arrive(gall, ga_s, ga_r, gf_s, gf_r, d)
        acc[...] += jnp.dot(ptc[p], gall[p], preferred_element_type=F32)
    for d in range(pairs_n):
        p = arrive2(gall, gf_s, gf_r, d)
        acc[...] += jnp.dot(ptc[p], gall[p], preferred_element_type=F32)
    php_out[...] = acc[...].T

    drain(mine, pall, pa_s, pa_r, pf_s, pf_r)
    drain(own, gall, ga_s, ga_r, gf_s, gf_r)
    for e in range(rows_n):
        for d in range(1, rows_n):
            cz_copy(e, d).wait_send()
    for d in range(rows_n):
        for up in (True, False):
            @pl.when(sends(d, up))
            def _():
                chain(d, up, False).wait_send()

            @pl.when(sends(d, up) & (source(d, up) == my_pair))
            def _():
                chain(d, up, True).wait_send()

    @pl.when(me_row != my_pair)
    def _():
        for d in range(1, rows_n):
            rest(d).wait_send()


def per_device(hamiltonian, pattern, tile_lists, orders, shift):
    rows_n = lax.axis_size("row")
    cols_n = lax.axis_size("col")
    high, wide = hamiltonian.shape
    groups = pattern.shape[0] // TPC
    gpr = high // TILE // TPC
    width = wide // rows_n
    pairs_n = cols_n // 2
    steps = jnp.arange(MAXT, dtype=jnp.int32)
    g = jnp.arange(groups, dtype=jnp.int32)
    hit = (tile_lists[:, None, :] // TPC == g[None, :, None]) & (
        steps[None, None, :] < orders[:, None, None])
    code = jnp.max(
        jnp.where(hit, steps[None, None, :] * TPC + tile_lists[:, None, :] % TPC, -1), axis=2)
    dma = pltpu.SemaphoreType.DMA
    smem = pl.BlockSpec(memory_space=pltpu.SMEM)
    vmem = pl.BlockSpec(memory_space=pltpu.VMEM)
    return pl.pallas_call(
        functools.partial(kernel, rows_n, cols_n),
        out_shape=(
            jax.ShapeDtypeStruct((high, wide), BF),
            jax.ShapeDtypeStruct((high, wide), F32),
        ),
        in_specs=[smem] * 5 + [vmem],
        out_specs=(vmem, vmem),
        scratch_shapes=[
            pltpu.VMEM((rows_n, high, wide), BF),
            pltpu.VMEM((cols_n, rows_n + 1, TILE, TILE), BF),
            pltpu.VMEM((cols_n, rows_n + 1, TILE, TILE), BF),
            pltpu.VMEM((SPAN, SPAN), BF),
            pltpu.VMEM((SPAN, SPAN), BF),
            pltpu.VMEM((SPAN, SPAN), BF),
            pltpu.VMEM((MAXT, TILE, TILE), BF),
            pltpu.VMEM((groups, wide, TILE), BF),
            pltpu.VMEM((cols_n, gpr, wide, TILE), BF),
            pltpu.VMEM((wide, high), BF),
            pltpu.VMEM((groups, wide, TPC * TILE), BF),
            pltpu.VMEM((cols_n, wide, high), BF),
            pltpu.VMEM((groups, wide, TPC * TILE), BF),
            pltpu.VMEM((wide, high), F32),
            *[dma((rows_n,))] * 10,
            dma((rows_n + 1, cols_n)), dma((rows_n + 1, cols_n)),
            dma((rows_n, rows_n)), dma((rows_n, rows_n)),
            dma((pairs_n,)), dma((pairs_n,)), dma((pairs_n,)), dma((pairs_n,)),
            dma((pairs_n,)), dma((pairs_n,)), dma((pairs_n,)), dma((pairs_n,)),
        ],
        compiler_params=pltpu.CompilerParams(
            collective_id=0, has_side_effects=True, vmem_limit_bytes=60000000),
    )(code, tile_lists, orders, pattern, shift, hamiltonian)


def solution(mesh):
    in_specs = (P("row", "col"), P(), P(), P(), P())
    out_specs = (P("row", "col"), P("row", "col"))
    return jax.shard_map(
        per_device, mesh=mesh, in_specs=in_specs, out_specs=out_specs, check_vma=False
    )
```

```python
import functools

import jax
import jax.numpy as jnp
from jax import lax
from jax.experimental import pallas as pl
from jax.experimental.pallas import tpu as pltpu
from jax.sharding import PartitionSpec as P

TILE = 128
TPC = 2
MAXT = 8
ITERS = 3
BF = jnp.bfloat16
F32 = jnp.float32
MESH = pl.DeviceIdType.MESH
SPAN = MAXT * TILE
BLOCK = 256


def eye_block(rows, cols, shift):
    r = lax.broadcasted_iota(jnp.int32, (rows, cols), 0)
    c = lax.broadcasted_iota(jnp.int32, (rows, cols), 1)
    return r == c + shift


def kernel(
    rows_n, cols_n, code, lists, orders, pattern, shift, ham,
    dens_out, php_out,
    strip, stage, arr, xa, fb, turned, cent, call, pall, pt, ptc, gall, ht, acc,
    az_s, az_r, bz_s, bz_r, aa_s, aa_r, cz_s, cz_r, pa_s, pa_r, pf_s, pf_r, ga_s, ga_r, gf_s, gf_r,
):
    me_row = lax.axis_index("row")
    me_col = lax.axis_index("col")
    high, wide = ham.shape
    row_tiles = high // TILE
    gpr = row_tiles // TPC
    groups = rows_n * gpr
    width = wide // rows_n
    pairs_n = cols_n // 2
    my_pair = me_col // 2
    parity = lax.rem(me_col, 2)
    partner = my_pair * 2 + 1 - parity
    solver = me_col * rows_n + me_row

    def send(src, dst, ss, rs, row, col):
        return pltpu.make_async_remote_copy(
            src_ref=src, dst_ref=dst, send_sem=ss, recv_sem=rs,
            device_id=(row, col), device_id_type=MESH,
        )

    barrier = pltpu.get_barrier_semaphore()
    for d in range(1, rows_n):
        pl.semaphore_signal(
            barrier, inc=1, device_id=(lax.rem(me_row + d, rows_n), me_col), device_id_type=MESH)
    for d in range(1, cols_n):
        pl.semaphore_signal(
            barrier, inc=1, device_id=(me_row, lax.rem(me_col + d, cols_n)), device_id_type=MESH)
    pl.semaphore_wait(barrier, rows_n - 1 + cols_n - 1)

    half_rows = TPC * TILE

    def first(q):
        return jnp.where(q == my_pair, 0, jnp.where(q < my_pair, parity, 1 - parity))

    def rows_of(half):
        return pl.ds(pl.multiple_of(half * half_rows, half_rows), half_rows)

    def piece(d, other):
        half = 1 - first(me_row) if other else first(me_row)
        ss, rs = (bz_s, bz_r) if other else (az_s, az_r)
        return send(ham.at[rows_of(half)], strip.at[me_row, rows_of(half)], ss.at[d], rs.at[d],
                    lax.rem(me_row + d, rows_n), me_col)

    def piece_in(d, other):
        q = lax.rem(me_row + rows_n - d, rows_n)
        ref = strip.at[q, rows_of(1 - first(q) if other else first(q))]
        ss, rs = (bz_s, bz_r) if other else (az_s, az_r)
        return send(ref, ref, ss.at[d], rs.at[d], lax.rem(me_row + d, rows_n), me_col)

    def pick(s, g):
        return lax.rem(jnp.maximum(code[s, g], 0), 2)

    def distribute(block, q, half, slot):
        g = q * gpr + half
        base = half * half_rows

        def one(d, carry):
            p = lax.rem(me_col + d, cols_n)
            s = p * rows_n + me_row
            right = pick(s, me_col) == 1
            low = pick(s, g) == 1
            above = pl.ds(pl.multiple_of(base, TILE), TILE)
            below = pl.ds(pl.multiple_of(base + TILE, TILE), TILE)
            top = jnp.where(right, block[above, TILE:2 * TILE], block[above, 0:TILE])
            bottom = jnp.where(right, block[below, TILE:2 * TILE], block[below, 0:TILE])
            tile = jnp.where(low, bottom, top)

            @pl.when(d > 0)
            def _():
                stage[p, slot] = tile
                send(stage.at[p, slot], arr.at[me_col, slot],
                     aa_s.at[slot, p], aa_r.at[slot, me_col], me_row, p).start()

            @pl.when(d == 0)
            def _():
                arr[me_col, slot] = tile
            return carry
        lax.fori_loop(0, cols_n, one, 0)

    def turn(block, q, half):
        for a in range(TPC):
            for b in range(TPC):
                ga = q * row_tiles + half * TPC + a
                gb = me_col * TPC + b
                keep = (pattern[ga, gb] == 1) | (ga == gb)
                rows = pl.ds(pl.multiple_of(half * half_rows + a * TILE, TILE), TILE)
                t = block[rows, b * TILE:(b + 1) * TILE]
                t = jnp.where(keep, t, jnp.zeros_like(t))
                ht[q * gpr + half, b * TILE:(b + 1) * TILE, a * TILE:(a + 1) * TILE] = t.T

    steps = [1, rows_n - 1] + list(range(2, rows_n - 1))
    for d in steps:
        piece(d, False).start()

    @pl.when(me_row == my_pair)
    def _():
        for d in steps:
            piece(d, True).start()

    distribute(ham, me_row, first(me_row), me_row)

    @pl.when(me_row == my_pair)
    def _():
        distribute(ham, me_row, 1 - first(me_row), rows_n)
    for d in steps:
        q = lax.rem(me_row + rows_n - d, rows_n)
        piece_in(d, False).wait_recv()
        distribute(strip.at[q], q, first(q), q)
    for d in steps:
        q = lax.rem(me_row + rows_n - d, rows_n)

        @pl.when(q == my_pair)
        def _():
            piece_in(d, True).wait_recv()
            distribute(strip.at[q], q, 1 - first(q), rows_n)

    turn(ham, me_row, 0)
    turn(ham, me_row, 1)

    def turn_other(d, carry):
        q = lax.rem(me_row + d, rows_n)
        turn(strip.at[q], q, first(q))
        return carry
    lax.fori_loop(1, rows_n, turn_other, 0)

    def wait_all(d, carry):
        p = lax.rem(me_col + d, cols_n)

        def inner(slot, c):
            send(stage.at[p, slot], arr.at[p, slot],
                 aa_s.at[slot, p], aa_r.at[slot, p], me_row, p).wait()
            return c
        return lax.fori_loop(0, rows_n + 1, inner, carry)
    lax.fori_loop(1, cols_n, wait_all, 0)

    @pl.when(me_row != my_pair)
    def _():
        for d in steps:
            piece(d, True).start()

    potential = shift[0]
    order = orders[solver]

    def slot_of(g, h):
        return jnp.where((g // TPC == h // TPC) & (lax.rem(g, TPC) == 1), rows_n, g // TPC)

    for i in range(MAXT):
        ti = lists[solver, i]
        gi = ti // TPC
        for j in range(i, MAXT):
            tj = lists[solver, j]
            gj = tj // TPC
            keep = (i < order) & (j < order)
            here = slice(i * TILE, (i + 1) * TILE)
            there = slice(j * TILE, (j + 1) * TILE)
            if i == j:
                t = arr[gi, slot_of(gi, gi)]
                xa[here, here] = jnp.where(keep, t, jnp.zeros_like(t))
                continue
            keep = keep & (pattern[ti, tj] == 1)
            even = lax.rem(gi + gj, 2) == 0
            ri, rj = gi // TPC, gj // TPC
            as_is = (ri == rj) | ((ri < rj) & even) | ((ri > rj) & jnp.logical_not(even))
            w = jnp.where(as_is, arr[gj, slot_of(gi, gj)], arr[gi, slot_of(gj, gi)])
            w = jnp.where(keep, w, jnp.zeros_like(w))
            wt = w.T
            xa[here, there] = jnp.where(as_is, w, wt)
            xa[there, here] = jnp.where(as_is, wt, w)

    def squares(i, most):
        v = xa[pl.ds(pl.multiple_of(i * TILE, TILE), TILE), :].astype(F32)
        move = jnp.where(i < order, potential, 0.0)
        v = v - jnp.where(eye_block(TILE, SPAN, 0 - i * TILE), move, 0.0)
        return jnp.maximum(most, jnp.sum(v * v, axis=1, keepdims=True))
    biggest = lax.fori_loop(0, MAXT, squares, jnp.zeros((TILE, 1), F32))
    top = jnp.max(biggest, axis=0, keepdims=True)
    scale = jnp.abs(potential) + 2.0 * jnp.sqrt(top + 1e-06)
    inverse = 1.0 / scale

    def norm(i, carry):
        rows = pl.ds(pl.multiple_of(i * TILE, TILE), TILE)
        v = xa[rows, :].astype(F32)
        hit = eye_block(TILE, SPAN, 0 - i * TILE)
        move = jnp.where(i < order, potential, 0.0)
        v = v - jnp.where(hit, move, 0.0)
        xa[rows, :] = (v * inverse).astype(BF)
        return carry
    lax.fori_loop(0, MAXT, norm, 0)

    x, f = xa, fb
    for step in range(ITERS - 1):
        y = turned

        def square(n, carry):
            cols = pl.ds(pl.multiple_of(n * BLOCK, BLOCK), BLOCK)
            q = jnp.dot(x[...], x[:, cols], preferred_element_type=F32)
            hit = eye_block(SPAN, BLOCK, n * BLOCK)
            f[:, cols] = (jnp.where(hit, 1.5, 0.0) - 0.5 * q).astype(BF)
            return carry
        lax.fori_loop(0, SPAN // BLOCK, square, 0)

        def times(n, carry):
            cols = pl.ds(pl.multiple_of(n * BLOCK, BLOCK), BLOCK)
            y[:, cols] = jnp.dot(x[...], f[:, cols], preferred_element_type=F32).astype(BF)
            return carry
        lax.fori_loop(0, SPAN // BLOCK, times, 0)
        x, turned = y, x
    q = jnp.dot(x[...], x[:, 0:TILE], preferred_element_type=F32)
    hit = eye_block(SPAN, TILE, 0)
    f[:, 0:TILE] = (jnp.where(hit, 1.5, 0.0) - 0.5 * q).astype(BF)
    y3 = jnp.dot(x[...], f[:, 0:TILE], preferred_element_type=F32)
    dens = (0.5 * (jnp.where(hit, 1.0, 0.0) - y3)).astype(BF)
    for i in range(MAXT):
        cent[i] = dens[i * TILE:(i + 1) * TILE, :].T

    offset = pl.multiple_of(lax.rem(solver * width, TILE), width)
    my_rows = pl.ds(pl.multiple_of(me_row * width, width), width)

    def place(g, carry):
        where = code[solver, g]
        t = cent[jnp.maximum(where, 0) // 2, pl.ds(offset, width), :]
        call[g, my_rows, :] = jnp.where(where >= 0, t, jnp.zeros_like(t))
        return carry
    lax.fori_loop(0, groups, place, 0)

    def cz_copy(e, d):
        to = lax.rem(me_row + d, rows_n)
        part = lax.rem(me_row + d + e, rows_n)
        part_ref = call.at[pl.ds(part * gpr, gpr), my_rows, :]
        return send(part_ref, part_ref, cz_s.at[e, d], cz_r.at[e, d], to, me_col)

    for e in range(rows_n):
        for d in range(1, rows_n):
            cz_copy(e, d).start()

    for d in steps:
        q = lax.rem(me_row + rows_n - d, rows_n)

        @pl.when(q != my_pair)
        def _():
            piece_in(d, True).wait_recv()
        turn(strip.at[q], q, 1 - first(q))
    for d in range(1, rows_n):
        cz_copy(0, d).wait_recv()

    mine = call.at[pl.ds(me_row * gpr, gpr)]

    def gather(src, buf, s1, r1, s2, r2):
        for d in range(1, pairs_n):
            p = lax.rem(my_pair + d, pairs_n) * 2 + parity
            send(src, buf.at[me_col], s1.at[d], r1.at[d], me_row, p).start()
        send(src, buf.at[me_col], s2.at[0], r2.at[0], me_row, partner).start()

    def arrive(buf, s1, r1, s2, r2, d):
        p = lax.rem(my_pair + pairs_n - d, pairs_n) * 2 + parity
        ref = buf.at[p]
        send(ref, ref, s1.at[d], r1.at[d], me_row, p).wait_recv()
        send(ref, ref, s2.at[d], r2.at[d], me_row, partner).start()
        return p

    def arrive2(buf, s2, r2, d):
        p = lax.rem(my_pair + pairs_n - d, pairs_n) * 2 + (1 - parity)
        ref = buf.at[p]
        send(ref, ref, s2.at[d], r2.at[d], me_row, partner).wait_recv()
        return p

    def drain(src, buf, s1, r1, s2, r2):
        for d in range(pairs_n):
            if d:
                send(src, buf.at[me_col], s1.at[d], r1.at[d], me_row, partner).wait_send()
            send(src, buf.at[me_col], s2.at[d], r2.at[d], me_row, partner).wait_send()

    gather(mine, pall, pa_s, pa_r, pf_s, pf_r)

    def spread(src, c):
        for q in range(rows_n):
            s = c * rows_n + q
            for t in range(row_tiles):
                cd = code[s, me_row * gpr + t // TPC]
                v = src[t // TPC, q * width:(q + 1) * width, :]
                ok = (cd >= 0) & (lax.rem(jnp.maximum(cd, 0), 2) == t % TPC)
                pt[q * width:(q + 1) * width, t * TILE:(t + 1) * TILE] = jnp.where(
                    ok, v, jnp.zeros_like(v))

    def term(src, c, first=False):
        spread(src, c)
        v = jnp.dot(ht[c], pt[...], preferred_element_type=F32)
        if first:
            acc[...] = v
        else:
            acc[...] += v

    term(mine, me_col, True)
    dens_out[...] = pt[...].T
    for d in range(1, pairs_n):
        p = arrive(pall, pa_s, pa_r, pf_s, pf_r, d)
        term(pall.at[p], p)
    for d in range(pairs_n):
        p = arrive2(pall, pf_s, pf_r, d)
        term(pall.at[p], p)
    gall[me_col] = acc[...].astype(BF)
    own = gall.at[me_col]
    gather(own, gall, ga_s, ga_r, gf_s, gf_r)

    for e in range(1, rows_n):
        for d in range(1, rows_n):
            cz_copy(e, d).wait_recv()
    for q in range(rows_n):
        s = me_col * rows_n + q
        for g in range(groups):
            cd = code[s, g]
            v = call[g, q * width:(q + 1) * width, :]
            for h in range(TPC):
                ok = (cd >= 0) & (lax.rem(jnp.maximum(cd, 0), 2) == h)
                ptc[g, q * width:(q + 1) * width,
                    h * TILE:(h + 1) * TILE] = jnp.where(ok, v, jnp.zeros_like(v))

    acc[...] = jnp.dot(ptc[me_col], own[...], preferred_element_type=F32)
    for d in range(1, pairs_n):
        p = arrive(gall, ga_s, ga_r, gf_s, gf_r, d)
        acc[...] += jnp.dot(ptc[p], gall[p], preferred_element_type=F32)
    for d in range(pairs_n):
        p = arrive2(gall, gf_s, gf_r, d)
        acc[...] += jnp.dot(ptc[p], gall[p], preferred_element_type=F32)
    php_out[...] = acc[...].T

    drain(mine, pall, pa_s, pa_r, pf_s, pf_r)
    drain(own, gall, ga_s, ga_r, gf_s, gf_r)
    for e in range(rows_n):
        for d in range(1, rows_n):
            cz_copy(e, d).wait_send()
    for d in steps:
        piece(d, False).wait_send()
        piece(d, True).wait_send()


def per_device(hamiltonian, pattern, tile_lists, orders, shift):
    rows_n = lax.axis_size("row")
    cols_n = lax.axis_size("col")
    high, wide = hamiltonian.shape
    groups = pattern.shape[0] // TPC
    gpr = high // TILE // TPC
    width = wide // rows_n
    pairs_n = cols_n // 2
    steps = jnp.arange(MAXT, dtype=jnp.int32)
    g = jnp.arange(groups, dtype=jnp.int32)
    hit = (tile_lists[:, None, :] // TPC == g[None, :, None]) & (
        steps[None, None, :] < orders[:, None, None])
    code = jnp.max(
        jnp.where(hit, steps[None, None, :] * TPC + tile_lists[:, None, :] % TPC, -1), axis=2)
    dma = pltpu.SemaphoreType.DMA
    smem = pl.BlockSpec(memory_space=pltpu.SMEM)
    vmem = pl.BlockSpec(memory_space=pltpu.VMEM)
    return pl.pallas_call(
        functools.partial(kernel, rows_n, cols_n),
        out_shape=(
            jax.ShapeDtypeStruct((high, wide), BF),
            jax.ShapeDtypeStruct((high, wide), F32),
        ),
        in_specs=[smem] * 5 + [vmem],
        out_specs=(vmem, vmem),
        scratch_shapes=[
            pltpu.VMEM((rows_n, high, wide), BF),
            pltpu.VMEM((cols_n, rows_n + 1, TILE, TILE), BF),
            pltpu.VMEM((cols_n, rows_n + 1, TILE, TILE), BF),
            pltpu.VMEM((SPAN, SPAN), BF),
            pltpu.VMEM((SPAN, SPAN), BF),
            pltpu.VMEM((SPAN, SPAN), BF),
            pltpu.VMEM((MAXT, TILE, TILE), BF),
            pltpu.VMEM((groups, wide, TILE), BF),
            pltpu.VMEM((cols_n, gpr, wide, TILE), BF),
            pltpu.VMEM((wide, high), BF),
            pltpu.VMEM((groups, wide, TPC * TILE), BF),
            pltpu.VMEM((cols_n, wide, high), BF),
            pltpu.VMEM((groups, wide, TPC * TILE), BF),
            pltpu.VMEM((wide, high), F32),
            *[dma((rows_n,))] * 4,
            dma((rows_n + 1, cols_n)), dma((rows_n + 1, cols_n)),
            dma((rows_n, rows_n)), dma((rows_n, rows_n)),
            dma((pairs_n,)), dma((pairs_n,)), dma((pairs_n,)), dma((pairs_n,)),
            dma((pairs_n,)), dma((pairs_n,)), dma((pairs_n,)), dma((pairs_n,)),
        ],
        compiler_params=pltpu.CompilerParams(
            collective_id=0, has_side_effects=True, vmem_limit_bytes=60000000),
    )(code, tile_lists, orders, pattern, shift, hamiltonian)


def solution(mesh):
    in_specs = (P("row", "col"), P(), P(), P(), P())
    out_specs = (P("row", "col"), P("row", "col"))
    return jax.shard_map(
        per_device, mesh=mesh, in_specs=in_specs, out_specs=out_specs, check_vma=False
    )
```

```python
import functools

import jax
import jax.numpy as jnp
from jax import lax
from jax.experimental import pallas as pl
from jax.experimental.pallas import tpu as pltpu
from jax.sharding import PartitionSpec as P

TILE = 128
TPC = 2
MAXT = 8
ITERS = 3
BF = jnp.bfloat16
F32 = jnp.float32
MESH = pl.DeviceIdType.MESH
SPAN = MAXT * TILE
BLOCK = 256


def eye_block(rows, cols, shift):
    r = lax.broadcasted_iota(jnp.int32, (rows, cols), 0)
    c = lax.broadcasted_iota(jnp.int32, (rows, cols), 1)
    return r == c + shift


def kernel(
    rows_n, cols_n, code, lists, orders, pattern, shift, ham,
    dens_out, php_out,
    strip, stage, arr, xa, fb, turned, cent, call, pall, pt, ptc, gall, ht, acc,
    az_s, az_r, bz_s, bz_r, aa_s, aa_r, cz_s, cz_r, pa_s, pa_r, ga_s, ga_r,
):
    me_row = lax.axis_index("row")
    me_col = lax.axis_index("col")
    high, wide = ham.shape
    row_tiles = high // TILE
    gpr = row_tiles // TPC
    groups = rows_n * gpr
    width = wide // rows_n
    pairs_n = cols_n // 2
    my_pair = me_col // 2
    parity = lax.rem(me_col, 2)
    partner = my_pair * 2 + 1 - parity
    solver = me_col * rows_n + me_row

    def send(src, dst, ss, rs, row, col):
        return pltpu.make_async_remote_copy(
            src_ref=src, dst_ref=dst, send_sem=ss, recv_sem=rs,
            device_id=(row, col), device_id_type=MESH,
        )

    barrier = pltpu.get_barrier_semaphore()
    for d in range(1, rows_n):
        pl.semaphore_signal(
            barrier, inc=1, device_id=(lax.rem(me_row + d, rows_n), me_col), device_id_type=MESH)
    for d in range(1, cols_n):
        pl.semaphore_signal(
            barrier, inc=1, device_id=(me_row, lax.rem(me_col + d, cols_n)), device_id_type=MESH)
    pl.semaphore_wait(barrier, rows_n - 1 + cols_n - 1)

    half_rows = TPC * TILE

    def first(q):
        return jnp.where(q == my_pair, 0, jnp.where(q < my_pair, parity, 1 - parity))

    def rows_of(half):
        return pl.ds(pl.multiple_of(half * half_rows, half_rows), half_rows)

    def piece(d, other):
        half = 1 - first(me_row) if other else first(me_row)
        ss, rs = (bz_s, bz_r) if other else (az_s, az_r)
        return send(ham.at[rows_of(half)], strip.at[me_row, rows_of(half)], ss.at[d], rs.at[d],
                    lax.rem(me_row + d, rows_n), me_col)

    def piece_in(d, other):
        q = lax.rem(me_row + rows_n - d, rows_n)
        ref = strip.at[q, rows_of(1 - first(q) if other else first(q))]
        ss, rs = (bz_s, bz_r) if other else (az_s, az_r)
        return send(ref, ref, ss.at[d], rs.at[d], lax.rem(me_row + d, rows_n), me_col)

    def pick(s, g):
        return lax.rem(jnp.maximum(code[s, g], 0), 2)

    def distribute(block, q, half, slot):
        g = q * gpr + half
        base = half * half_rows

        def one(d, carry):
            p = lax.rem(me_col + d, cols_n)
            s = p * rows_n + me_row
            right = pick(s, me_col) == 1
            low = pick(s, g) == 1
            above = pl.ds(pl.multiple_of(base, TILE), TILE)
            below = pl.ds(pl.multiple_of(base + TILE, TILE), TILE)
            top = jnp.where(right, block[above, TILE:2 * TILE], block[above, 0:TILE])
            bottom = jnp.where(right, block[below, TILE:2 * TILE], block[below, 0:TILE])
            tile = jnp.where(low, bottom, top)

            @pl.when(d > 0)
            def _():
                stage[p, slot] = tile
                send(stage.at[p, slot], arr.at[me_col, slot],
                     aa_s.at[slot, p], aa_r.at[slot, me_col], me_row, p).start()

            @pl.when(d == 0)
            def _():
                arr[me_col, slot] = tile
            return carry
        lax.fori_loop(0, cols_n, one, 0)

    def turn(block, q, half):
        for a in range(TPC):
            for b in range(TPC):
                ga = q * row_tiles + half * TPC + a
                gb = me_col * TPC + b
                keep = (pattern[ga, gb] == 1) | (ga == gb)
                rows = pl.ds(pl.multiple_of(half * half_rows + a * TILE, TILE), TILE)
                t = block[rows, b * TILE:(b + 1) * TILE]
                t = jnp.where(keep, t, jnp.zeros_like(t))
                ht[q * gpr + half, b * TILE:(b + 1) * TILE, a * TILE:(a + 1) * TILE] = t.T

    steps = [1, rows_n - 1] + list(range(2, rows_n - 1))
    for d in steps:
        piece(d, False).start()

    @pl.when(me_row == my_pair)
    def _():
        for d in steps:
            piece(d, True).start()

    distribute(ham, me_row, first(me_row), me_row)

    @pl.when(me_row == my_pair)
    def _():
        distribute(ham, me_row, 1 - first(me_row), rows_n)
    for d in steps:
        q = lax.rem(me_row + rows_n - d, rows_n)
        piece_in(d, False).wait_recv()
        distribute(strip.at[q], q, first(q), q)
    for d in steps:
        q = lax.rem(me_row + rows_n - d, rows_n)

        @pl.when(q == my_pair)
        def _():
            piece_in(d, True).wait_recv()
            distribute(strip.at[q], q, 1 - first(q), rows_n)

    turn(ham, me_row, 0)
    turn(ham, me_row, 1)

    def turn_other(d, carry):
        q = lax.rem(me_row + d, rows_n)
        turn(strip.at[q], q, first(q))
        return carry
    lax.fori_loop(1, rows_n, turn_other, 0)

    def wait_all(d, carry):
        p = lax.rem(me_col + d, cols_n)

        def inner(slot, c):
            send(stage.at[p, slot], arr.at[p, slot],
                 aa_s.at[slot, p], aa_r.at[slot, p], me_row, p).wait()
            return c
        return lax.fori_loop(0, rows_n + 1, inner, carry)
    lax.fori_loop(1, cols_n, wait_all, 0)

    @pl.when(me_row != my_pair)
    def _():
        for d in steps:
            piece(d, True).start()

    potential = shift[0]
    order = orders[solver]

    def slot_of(g, h):
        return jnp.where((g // TPC == h // TPC) & (lax.rem(g, TPC) == 1), rows_n, g // TPC)

    for i in range(MAXT):
        ti = lists[solver, i]
        gi = ti // TPC
        for j in range(i, MAXT):
            tj = lists[solver, j]
            gj = tj // TPC
            keep = (i < order) & (j < order)
            here = slice(i * TILE, (i + 1) * TILE)
            there = slice(j * TILE, (j + 1) * TILE)
            if i == j:
                t = arr[gi, slot_of(gi, gi)]
                xa[here, here] = jnp.where(keep, t, jnp.zeros_like(t))
                continue
            keep = keep & (pattern[ti, tj] == 1)
            even = lax.rem(gi + gj, 2) == 0
            ri, rj = gi // TPC, gj // TPC
            as_is = (ri == rj) | ((ri < rj) & even) | ((ri > rj) & jnp.logical_not(even))
            w = jnp.where(as_is, arr[gj, slot_of(gi, gj)], arr[gi, slot_of(gj, gi)])
            w = jnp.where(keep, w, jnp.zeros_like(w))
            wt = w.T
            xa[here, there] = jnp.where(as_is, w, wt)
            xa[there, here] = jnp.where(as_is, wt, w)

    def squares(i, most):
        v = xa[pl.ds(pl.multiple_of(i * TILE, TILE), TILE), :].astype(F32)
        move = jnp.where(i < order, potential, 0.0)
        v = v - jnp.where(eye_block(TILE, SPAN, 0 - i * TILE), move, 0.0)
        return jnp.maximum(most, jnp.sum(v * v, axis=1, keepdims=True))
    biggest = lax.fori_loop(0, MAXT, squares, jnp.zeros((TILE, 1), F32))
    top = jnp.max(biggest, axis=0, keepdims=True)
    scale = jnp.abs(potential) + 2.0 * jnp.sqrt(top + 1e-06)
    inverse = 1.0 / scale

    def norm(i, carry):
        rows = pl.ds(pl.multiple_of(i * TILE, TILE), TILE)
        v = xa[rows, :].astype(F32)
        hit = eye_block(TILE, SPAN, 0 - i * TILE)
        move = jnp.where(i < order, potential, 0.0)
        v = v - jnp.where(hit, move, 0.0)
        xa[rows, :] = (v * inverse).astype(BF)
        return carry
    lax.fori_loop(0, MAXT, norm, 0)

    x, f = xa, fb
    for step in range(ITERS - 1):
        y = turned

        def square(n, carry):
            cols = pl.ds(pl.multiple_of(n * BLOCK, BLOCK), BLOCK)
            q = jnp.dot(x[...], x[:, cols], preferred_element_type=F32)
            hit = eye_block(SPAN, BLOCK, n * BLOCK)
            f[:, cols] = (jnp.where(hit, 1.5, 0.0) - 0.5 * q).astype(BF)
            return carry
        lax.fori_loop(0, SPAN // BLOCK, square, 0)

        def times(n, carry):
            cols = pl.ds(pl.multiple_of(n * BLOCK, BLOCK), BLOCK)
            y[:, cols] = jnp.dot(x[...], f[:, cols], preferred_element_type=F32).astype(BF)
            return carry
        lax.fori_loop(0, SPAN // BLOCK, times, 0)
        x, turned = y, x
    q = jnp.dot(x[...], x[:, 0:TILE], preferred_element_type=F32)
    hit = eye_block(SPAN, TILE, 0)
    f[:, 0:TILE] = (jnp.where(hit, 1.5, 0.0) - 0.5 * q).astype(BF)
    y3 = jnp.dot(x[...], f[:, 0:TILE], preferred_element_type=F32)
    dens = (0.5 * (jnp.where(hit, 1.0, 0.0) - y3)).astype(BF)
    for i in range(MAXT):
        cent[i] = dens[i * TILE:(i + 1) * TILE, :].T

    offset = pl.multiple_of(lax.rem(solver * width, TILE), width)
    my_rows = pl.ds(pl.multiple_of(me_row * width, width), width)

    def place(g, carry):
        where = code[solver, g]
        t = cent[jnp.maximum(where, 0) // 2, pl.ds(offset, width), :]
        call[g, my_rows, :] = jnp.where(where >= 0, t, jnp.zeros_like(t))
        return carry
    lax.fori_loop(0, groups, place, 0)

    def cz_copy(e, d):
        to = lax.rem(me_row + d, rows_n)
        part = lax.rem(me_row + d + e, rows_n)
        part_ref = call.at[pl.ds(part * gpr, gpr), my_rows, :]
        return send(part_ref, part_ref, cz_s.at[e, d], cz_r.at[e, d], to, me_col)

    for e in range(rows_n):
        for d in range(1, rows_n):
            cz_copy(e, d).start()

    for d in steps:
        q = lax.rem(me_row + rows_n - d, rows_n)

        @pl.when(q != my_pair)
        def _():
            piece_in(d, True).wait_recv()
        turn(strip.at[q], q, 1 - first(q))
    for d in range(1, rows_n):
        cz_copy(0, d).wait_recv()

    relay = pairs_n == 4

    def flip(e):
        out, unit = 0, 1
        while unit < pairs_n:
            bit = lax.rem(my_pair // unit, 2)
            out = out + unit * (1 - bit if (e // unit) % 2 else bit)
            unit *= 2
        return out

    def net(src, buf, ss, rs, c, u, e, via):
        return send(src, buf.at[c, u], ss.at[e, u], rs.at[e, u], me_row, flip(via) * 2 + parity)

    def pass_on(src, buf, ss, rs, c, u, e):
        return send(src, buf.at[c, u], ss.at[pairs_n + e, u], rs.at[pairs_n + e, u],
                    me_row, partner)

    def start_own(src, buf, ss, rs, u):
        for e in range(1, 3 if relay else pairs_n):
            net(src, buf, ss, rs, me_col, u, e, e).start()
        pass_on(src, buf, ss, rs, me_col, u, 0).start()

    def from_net(buf, ss, rs, u, e):
        c = flip(e) * 2 + parity
        ref = buf.at[c, u]
        net(ref, buf, ss, rs, c, u, e, e).wait_recv()
        if relay and (u, e) == (0, 1):
            net(ref, buf, ss, rs, c, u, 3, 2).start()
        if relay and (u, e) == (1, 2):
            net(ref, buf, ss, rs, c, u, 3, 1).start()
        pass_on(ref, buf, ss, rs, c, u, e).start()
        return c

    def from_partner(buf, ss, rs, u, e):
        c = flip(e) * 2 + 1 - parity
        ref = buf.at[c, u]
        pass_on(ref, buf, ss, rs, c, u, e).wait_recv()
        return c

    def consume(buf, ss, rs, u, use):
        last = pairs_n - 1
        near = [from_net(buf, ss, rs, u, e) for e in range(1, last)]
        for c in near:
            use(c)
        use(from_partner(buf, ss, rs, u, 0))
        for e in range(1, last):
            use(from_partner(buf, ss, rs, u, e))
        use(from_net(buf, ss, rs, u, last))
        use(from_partner(buf, ss, rs, u, last))

    def drain(buf, ss, rs):
        for u in range(gpr):
            ref = buf.at[me_col, u]
            for e in range(pairs_n):
                if e:
                    net(ref, buf, ss, rs, me_col, u, e, e).wait_send()
                pass_on(ref, buf, ss, rs, me_col, u, e).wait_send()

    for u in range(gpr):
        start_own(call.at[me_row * gpr + u], pall, pa_s, pa_r, u)

    def spread(src, c, u):
        for q in range(rows_n):
            cd = code[c * rows_n + q, me_row * gpr + u]
            v = src[q * width:(q + 1) * width, :]
            for h in range(TPC):
                ok = (cd >= 0) & (lax.rem(jnp.maximum(cd, 0), 2) == h)
                pt[q * width:(q + 1) * width, h * TILE:(h + 1) * TILE] = jnp.where(
                    ok, v, jnp.zeros_like(v))

    for u in range(gpr):
        rows = slice(u * half_rows, (u + 1) * half_rows)
        spread(call.at[me_row * gpr + u], me_col, u)
        dens_out[rows, :] = pt[...].T
        acc[...] = jnp.dot(ht[me_col], pt[...], preferred_element_type=F32)

        def term(c):
            spread(pall.at[c, u], c, u)
            acc[...] += jnp.dot(ht[c], pt[...], preferred_element_type=F32)
        consume(pall, pa_s, pa_r, u, term)
        gall[me_col, u] = acc[...].astype(BF)
        start_own(gall.at[me_col, u], gall, ga_s, ga_r, u)

    for e in range(1, rows_n):
        for d in range(1, rows_n):
            cz_copy(e, d).wait_recv()
    for q in range(rows_n):
        s = me_col * rows_n + q
        for g in range(groups):
            cd = code[s, g]
            v = call[g, q * width:(q + 1) * width, :]
            for h in range(TPC):
                ok = (cd >= 0) & (lax.rem(jnp.maximum(cd, 0), 2) == h)
                ptc[g, q * width:(q + 1) * width, h * TILE:(h + 1) * TILE] = jnp.where(
                    ok, v, jnp.zeros_like(v))

    for u in range(gpr):
        acc[...] = jnp.dot(ptc[me_col], gall[me_col, u], preferred_element_type=F32)

        def last_term(c):
            acc[...] += jnp.dot(ptc[c], gall[c, u], preferred_element_type=F32)
        consume(gall, ga_s, ga_r, u, last_term)
        php_out[u * half_rows:(u + 1) * half_rows, :] = acc[...].T

    drain(pall, pa_s, pa_r)
    drain(gall, ga_s, ga_r)
    for e in range(rows_n):
        for d in range(1, rows_n):
            cz_copy(e, d).wait_send()
    for d in steps:
        piece(d, False).wait_send()
        piece(d, True).wait_send()


def per_device(hamiltonian, pattern, tile_lists, orders, shift):
    rows_n = lax.axis_size("row")
    cols_n = lax.axis_size("col")
    high, wide = hamiltonian.shape
    groups = pattern.shape[0] // TPC
    gpr = high // TILE // TPC
    width = wide // rows_n
    pairs_n = cols_n // 2
    steps = jnp.arange(MAXT, dtype=jnp.int32)
    g = jnp.arange(groups, dtype=jnp.int32)
    hit = (tile_lists[:, None, :] // TPC == g[None, :, None]) & (
        steps[None, None, :] < orders[:, None, None])
    code = jnp.max(
        jnp.where(hit, steps[None, None, :] * TPC + tile_lists[:, None, :] % TPC, -1), axis=2)
    dma = pltpu.SemaphoreType.DMA
    smem = pl.BlockSpec(memory_space=pltpu.SMEM)
    vmem = pl.BlockSpec(memory_space=pltpu.VMEM)
    return pl.pallas_call(
        functools.partial(kernel, rows_n, cols_n),
        out_shape=(
            jax.ShapeDtypeStruct((high, wide), BF),
            jax.ShapeDtypeStruct((high, wide), F32),
        ),
        in_specs=[smem] * 5 + [vmem],
        out_specs=(vmem, vmem),
        scratch_shapes=[
            pltpu.VMEM((rows_n, high, wide), BF),
            pltpu.VMEM((cols_n, rows_n + 1, TILE, TILE), BF),
            pltpu.VMEM((cols_n, rows_n + 1, TILE, TILE), BF),
            pltpu.VMEM((SPAN, SPAN), BF),
            pltpu.VMEM((SPAN, SPAN), BF),
            pltpu.VMEM((SPAN, SPAN), BF),
            pltpu.VMEM((MAXT, TILE, TILE), BF),
            pltpu.VMEM((groups, wide, TILE), BF),
            pltpu.VMEM((cols_n, gpr, wide, TILE), BF),
            pltpu.VMEM((wide, TPC * TILE), BF),
            pltpu.VMEM((groups, wide, TPC * TILE), BF),
            pltpu.VMEM((cols_n, gpr, wide, TPC * TILE), BF),
            pltpu.VMEM((groups, wide, TPC * TILE), BF),
            pltpu.VMEM((wide, TPC * TILE), F32),
            *[dma((rows_n,))] * 4,
            dma((rows_n + 1, cols_n)), dma((rows_n + 1, cols_n)),
            dma((rows_n, rows_n)), dma((rows_n, rows_n)),
            *[dma((2 * pairs_n, gpr))] * 4,
        ],
        compiler_params=pltpu.CompilerParams(
            collective_id=0, has_side_effects=True, vmem_limit_bytes=60000000),
    )(code, tile_lists, orders, pattern, shift, hamiltonian)


def solution(mesh):
    in_specs = (P("row", "col"), P(), P(), P(), P())
    out_specs = (P("row", "col"), P("row", "col"))
    return jax.shard_map(
        per_device, mesh=mesh, in_specs=in_specs, out_specs=out_specs, check_vma=False
    )
```

```python
import functools

import jax
import jax.numpy as jnp
from jax import lax
from jax.experimental import pallas as pl
from jax.experimental.pallas import tpu as pltpu
from jax.sharding import PartitionSpec as P

TILE = 128
TPC = 2
MAXT = 8
ITERS = 3
BF = jnp.bfloat16
F32 = jnp.float32
MESH = pl.DeviceIdType.MESH
SPAN = MAXT * TILE
BLOCK = 256


def eye_block(rows, cols, shift):
    r = lax.broadcasted_iota(jnp.int32, (rows, cols), 0)
    c = lax.broadcasted_iota(jnp.int32, (rows, cols), 1)
    return r == c + shift


def kernel(
    rows_n, cols_n, code, lists, orders, pattern, shift, ham,
    dens_out, php_out,
    strip, stage, arr, xa, fb, turned, cent, call, pall, pt, ptc, gall, ht, acc,
    az_s, az_r, bz_s, bz_r, aa_s, aa_r, cz_s, cz_r, pa_s, pa_r, ga_s, ga_r,
):
    me_row = lax.axis_index("row")
    me_col = lax.axis_index("col")
    high, wide = ham.shape
    row_tiles = high // TILE
    gpr = row_tiles // TPC
    groups = rows_n * gpr
    width = wide // rows_n
    pairs_n = cols_n // 2
    my_pair = me_col // 2
    parity = lax.rem(me_col, 2)
    partner = my_pair * 2 + 1 - parity
    solver = me_col * rows_n + me_row

    def send(src, dst, ss, rs, row, col):
        return pltpu.make_async_remote_copy(
            src_ref=src, dst_ref=dst, send_sem=ss, recv_sem=rs,
            device_id=(row, col), device_id_type=MESH,
        )

    barrier = pltpu.get_barrier_semaphore()
    for d in range(1, rows_n):
        pl.semaphore_signal(
            barrier, inc=1, device_id=(lax.rem(me_row + d, rows_n), me_col), device_id_type=MESH)
    for d in range(1, cols_n):
        pl.semaphore_signal(
            barrier, inc=1, device_id=(me_row, lax.rem(me_col + d, cols_n)), device_id_type=MESH)
    pl.semaphore_wait(barrier, rows_n - 1 + cols_n - 1)

    half_rows = TPC * TILE

    def first(q):
        return jnp.where(q == my_pair, 0, jnp.where(q < my_pair, parity, 1 - parity))

    def rows_of(half):
        return pl.ds(pl.multiple_of(half * half_rows, half_rows), half_rows)

    def piece(d, other):
        half = 1 - first(me_row) if other else first(me_row)
        ss, rs = (bz_s, bz_r) if other else (az_s, az_r)
        return send(ham.at[rows_of(half)], strip.at[me_row, rows_of(half)], ss.at[d], rs.at[d],
                    lax.rem(me_row + d, rows_n), me_col)

    def piece_in(d, other):
        q = lax.rem(me_row + rows_n - d, rows_n)
        ref = strip.at[q, rows_of(1 - first(q) if other else first(q))]
        ss, rs = (bz_s, bz_r) if other else (az_s, az_r)
        return send(ref, ref, ss.at[d], rs.at[d], lax.rem(me_row + d, rows_n), me_col)

    def pick(s, g):
        return lax.rem(jnp.maximum(code[s, g], 0), 2)

    def distribute(block, q, half, slot):
        g = q * gpr + half
        base = half * half_rows

        def one(d, carry):
            p = lax.rem(me_col + d, cols_n)
            s = p * rows_n + me_row
            right = pick(s, me_col) == 1
            low = pick(s, g) == 1
            above = pl.ds(pl.multiple_of(base, TILE), TILE)
            below = pl.ds(pl.multiple_of(base + TILE, TILE), TILE)
            top = jnp.where(right, block[above, TILE:2 * TILE], block[above, 0:TILE])
            bottom = jnp.where(right, block[below, TILE:2 * TILE], block[below, 0:TILE])
            tile = jnp.where(low, bottom, top)

            @pl.when(d > 0)
            def _():
                stage[p, slot] = tile
                send(stage.at[p, slot], arr.at[me_col, slot],
                     aa_s.at[slot, p], aa_r.at[slot, me_col], me_row, p).start()

            @pl.when(d == 0)
            def _():
                arr[me_col, slot] = tile
            return carry
        lax.fori_loop(0, cols_n, one, 0)

    def turn(block, q, half):
        for a in range(TPC):
            for b in range(TPC):
                ga = q * row_tiles + half * TPC + a
                gb = me_col * TPC + b
                keep = (pattern[ga, gb] == 1) | (ga == gb)
                rows = pl.ds(pl.multiple_of(half * half_rows + a * TILE, TILE), TILE)
                t = block[rows, b * TILE:(b + 1) * TILE]
                t = jnp.where(keep, t, jnp.zeros_like(t))
                ht[q * gpr + half, b * TILE:(b + 1) * TILE, a * TILE:(a + 1) * TILE] = t.T

    steps = [1, rows_n - 1] + list(range(2, rows_n - 1))
    for d in steps:
        piece(d, False).start()

    @pl.when(me_row == my_pair)
    def _():
        for d in steps:
            piece(d, True).start()

    distribute(ham, me_row, first(me_row), me_row)

    @pl.when(me_row == my_pair)
    def _():
        distribute(ham, me_row, 1 - first(me_row), rows_n)
    for d in steps:
        q = lax.rem(me_row + rows_n - d, rows_n)
        piece_in(d, False).wait_recv()
        distribute(strip.at[q], q, first(q), q)
    for d in steps:
        q = lax.rem(me_row + rows_n - d, rows_n)

        @pl.when(q == my_pair)
        def _():
            piece_in(d, True).wait_recv()
            distribute(strip.at[q], q, 1 - first(q), rows_n)

    turn(ham, me_row, 0)
    turn(ham, me_row, 1)

    def turn_other(d, carry):
        q = lax.rem(me_row + d, rows_n)
        turn(strip.at[q], q, first(q))
        return carry
    lax.fori_loop(1, rows_n, turn_other, 0)

    def wait_all(d, carry):
        p = lax.rem(me_col + d, cols_n)

        def inner(slot, c):
            send(stage.at[p, slot], arr.at[p, slot],
                 aa_s.at[slot, p], aa_r.at[slot, p], me_row, p).wait()
            return c
        return lax.fori_loop(0, rows_n + 1, inner, carry)
    lax.fori_loop(1, cols_n, wait_all, 0)

    @pl.when(me_row != my_pair)
    def _():
        for d in steps:
            piece(d, True).start()

    potential = shift[0]
    order = orders[solver]

    def slot_of(g, h):
        return jnp.where((g // TPC == h // TPC) & (lax.rem(g, TPC) == 1), rows_n, g // TPC)

    for i in range(MAXT):
        ti = lists[solver, i]
        gi = ti // TPC
        for j in range(i, MAXT):
            tj = lists[solver, j]
            gj = tj // TPC
            keep = (i < order) & (j < order)
            here = slice(i * TILE, (i + 1) * TILE)
            there = slice(j * TILE, (j + 1) * TILE)
            if i == j:
                t = arr[gi, slot_of(gi, gi)]
                xa[here, here] = jnp.where(keep, t, jnp.zeros_like(t))
                continue
            keep = keep & (pattern[ti, tj] == 1)
            even = lax.rem(gi + gj, 2) == 0
            ri, rj = gi // TPC, gj // TPC
            as_is = (ri == rj) | ((ri < rj) & even) | ((ri > rj) & jnp.logical_not(even))
            w = jnp.where(as_is, arr[gj, slot_of(gi, gj)], arr[gi, slot_of(gj, gi)])
            w = jnp.where(keep, w, jnp.zeros_like(w))
            wt = w.T
            xa[here, there] = jnp.where(as_is, w, wt)
            xa[there, here] = jnp.where(as_is, wt, w)

    def squares(i, most):
        v = xa[pl.ds(pl.multiple_of(i * TILE, TILE), TILE), :].astype(F32)
        move = jnp.where(i < order, potential, 0.0)
        v = v - jnp.where(eye_block(TILE, SPAN, 0 - i * TILE), move, 0.0)
        return jnp.maximum(most, jnp.sum(v * v, axis=1, keepdims=True))
    biggest = lax.fori_loop(0, MAXT, squares, jnp.zeros((TILE, 1), F32))
    top = jnp.max(biggest, axis=0, keepdims=True)
    scale = jnp.abs(potential) + 2.0 * jnp.sqrt(top + 1e-06)
    inverse = 1.0 / scale

    def norm(i, carry):
        rows = pl.ds(pl.multiple_of(i * TILE, TILE), TILE)
        v = xa[rows, :].astype(F32)
        hit = eye_block(TILE, SPAN, 0 - i * TILE)
        move = jnp.where(i < order, potential, 0.0)
        v = v - jnp.where(hit, move, 0.0)
        xa[rows, :] = (v * inverse).astype(BF)
        return carry
    lax.fori_loop(0, MAXT, norm, 0)

    x, f = xa, fb
    for step in range(ITERS - 1):
        y = turned

        def square(n, carry):
            cols = pl.ds(pl.multiple_of(n * BLOCK, BLOCK), BLOCK)
            q = jnp.dot(x[...], x[:, cols], preferred_element_type=F32)
            hit = eye_block(SPAN, BLOCK, n * BLOCK)
            f[:, cols] = (jnp.where(hit, 1.5, 0.0) - 0.5 * q).astype(BF)
            return carry
        lax.fori_loop(0, SPAN // BLOCK, square, 0)

        def times(n, carry):
            cols = pl.ds(pl.multiple_of(n * BLOCK, BLOCK), BLOCK)
            y[:, cols] = jnp.dot(x[...], f[:, cols], preferred_element_type=F32).astype(BF)
            return carry
        lax.fori_loop(0, SPAN // BLOCK, times, 0)
        x, turned = y, x
    q = jnp.dot(x[...], x[:, 0:TILE], preferred_element_type=F32)
    hit = eye_block(SPAN, TILE, 0)
    f[:, 0:TILE] = (jnp.where(hit, 1.5, 0.0) - 0.5 * q).astype(BF)
    y3 = jnp.dot(x[...], f[:, 0:TILE], preferred_element_type=F32)
    dens = (0.5 * (jnp.where(hit, 1.0, 0.0) - y3)).astype(BF)
    for i in range(MAXT):
        cent[i] = dens[i * TILE:(i + 1) * TILE, :].T

    offset = pl.multiple_of(lax.rem(solver * width, TILE), width)
    my_rows = pl.ds(pl.multiple_of(me_row * width, width), width)

    def place(g, carry):
        where = code[solver, g]
        t = cent[jnp.maximum(where, 0) // 2, pl.ds(offset, width), :]
        call[g, my_rows, :] = jnp.where(where >= 0, t, jnp.zeros_like(t))
        return carry
    lax.fori_loop(0, groups, place, 0)

    def cz_copy(e, d):
        to = lax.rem(me_row + d, rows_n)
        part = lax.rem(me_row + d + e, rows_n)
        part_ref = call.at[pl.ds(part * gpr, gpr), my_rows, :]
        return send(part_ref, part_ref, cz_s.at[e, d], cz_r.at[e, d], to, me_col)

    for e in range(rows_n):
        for d in range(1, rows_n):
            cz_copy(e, d).start()

    for d in steps:
        q = lax.rem(me_row + rows_n - d, rows_n)

        @pl.when(q != my_pair)
        def _():
            piece_in(d, True).wait_recv()
        turn(strip.at[q], q, 1 - first(q))
    for d in range(1, rows_n):
        cz_copy(0, d).wait_recv()


    def flip(e):
        out, unit = 0, 1
        while unit < pairs_n:
            bit = lax.rem(my_pair // unit, 2)
            out = out + unit * (1 - bit if (e // unit) % 2 else bit)
            unit *= 2
        return out

    def net(src, buf, ss, rs, c, u, e, via):
        return send(src, buf.at[c, u], ss.at[e, u], rs.at[e, u], me_row, flip(via) * 2 + parity)

    def pass_on(src, buf, ss, rs, c, u, e):
        return send(src, buf.at[c, u], ss.at[pairs_n + e, u], rs.at[pairs_n + e, u],
                    me_row, partner)

    def start_own(src, buf, ss, rs, u):
        for e in range(1, pairs_n):
            net(src, buf, ss, rs, me_col, u, e, e).start()
        pass_on(src, buf, ss, rs, me_col, u, 0).start()

    def from_net(buf, ss, rs, u, e):
        c = flip(e) * 2 + parity
        ref = buf.at[c, u]
        net(ref, buf, ss, rs, c, u, e, e).wait_recv()
        pass_on(ref, buf, ss, rs, c, u, e).start()
        return c

    def from_partner(buf, ss, rs, u, e):
        c = flip(e) * 2 + 1 - parity
        ref = buf.at[c, u]
        pass_on(ref, buf, ss, rs, c, u, e).wait_recv()
        return c

    def consume(buf, ss, rs, u, use):
        last = pairs_n - 1
        near = [from_net(buf, ss, rs, u, e) for e in range(1, last)]
        for c in near:
            use(c)
        use(from_partner(buf, ss, rs, u, 0))
        for e in range(1, last):
            use(from_partner(buf, ss, rs, u, e))
        use(from_net(buf, ss, rs, u, last))
        use(from_partner(buf, ss, rs, u, last))

    def drain(buf, ss, rs):
        for u in range(gpr):
            ref = buf.at[me_col, u]
            for e in range(pairs_n):
                if e:
                    net(ref, buf, ss, rs, me_col, u, e, e).wait_send()
                pass_on(ref, buf, ss, rs, me_col, u, e).wait_send()

    for u in range(gpr):
        start_own(call.at[me_row * gpr + u], pall, pa_s, pa_r, u)

    def spread(src, c, u):
        for q in range(rows_n):
            cd = code[c * rows_n + q, me_row * gpr + u]
            v = src[q * width:(q + 1) * width, :]
            for h in range(TPC):
                ok = (cd >= 0) & (lax.rem(jnp.maximum(cd, 0), 2) == h)
                pt[q * width:(q + 1) * width, h * TILE:(h + 1) * TILE] = jnp.where(
                    ok, v, jnp.zeros_like(v))

    for u in range(gpr):
        rows = slice(u * half_rows, (u + 1) * half_rows)
        spread(call.at[me_row * gpr + u], me_col, u)
        dens_out[rows, :] = pt[...].T
        acc[...] = jnp.dot(ht[me_col], pt[...], preferred_element_type=F32)

        def term(c):
            spread(pall.at[c, u], c, u)
            acc[...] += jnp.dot(ht[c], pt[...], preferred_element_type=F32)
        consume(pall, pa_s, pa_r, u, term)
        gall[me_col, u] = acc[...].astype(BF)
        start_own(gall.at[me_col, u], gall, ga_s, ga_r, u)

    for e in range(1, rows_n):
        for d in range(1, rows_n):
            cz_copy(e, d).wait_recv()
    for q in range(rows_n):
        s = me_col * rows_n + q
        for g in range(groups):
            cd = code[s, g]
            v = call[g, q * width:(q + 1) * width, :]
            for h in range(TPC):
                ok = (cd >= 0) & (lax.rem(jnp.maximum(cd, 0), 2) == h)
                ptc[g, q * width:(q + 1) * width, h * TILE:(h + 1) * TILE] = jnp.where(
                    ok, v, jnp.zeros_like(v))

    for u in range(gpr):
        acc[...] = jnp.dot(ptc[me_col], gall[me_col, u], preferred_element_type=F32)

        def last_term(c):
            acc[...] += jnp.dot(ptc[c], gall[c, u], preferred_element_type=F32)
        consume(gall, ga_s, ga_r, u, last_term)
        php_out[u * half_rows:(u + 1) * half_rows, :] = acc[...].T

    drain(pall, pa_s, pa_r)
    drain(gall, ga_s, ga_r)
    for e in range(rows_n):
        for d in range(1, rows_n):
            cz_copy(e, d).wait_send()
    for d in steps:
        piece(d, False).wait_send()
        piece(d, True).wait_send()


def per_device(hamiltonian, pattern, tile_lists, orders, shift):
    rows_n = lax.axis_size("row")
    cols_n = lax.axis_size("col")
    high, wide = hamiltonian.shape
    groups = pattern.shape[0] // TPC
    gpr = high // TILE // TPC
    width = wide // rows_n
    pairs_n = cols_n // 2
    steps = jnp.arange(MAXT, dtype=jnp.int32)
    g = jnp.arange(groups, dtype=jnp.int32)
    hit = (tile_lists[:, None, :] // TPC == g[None, :, None]) & (
        steps[None, None, :] < orders[:, None, None])
    code = jnp.max(
        jnp.where(hit, steps[None, None, :] * TPC + tile_lists[:, None, :] % TPC, -1), axis=2)
    dma = pltpu.SemaphoreType.DMA
    smem = pl.BlockSpec(memory_space=pltpu.SMEM)
    vmem = pl.BlockSpec(memory_space=pltpu.VMEM)
    return pl.pallas_call(
        functools.partial(kernel, rows_n, cols_n),
        out_shape=(
            jax.ShapeDtypeStruct((high, wide), BF),
            jax.ShapeDtypeStruct((high, wide), F32),
        ),
        in_specs=[smem] * 5 + [vmem],
        out_specs=(vmem, vmem),
        scratch_shapes=[
            pltpu.VMEM((rows_n, high, wide), BF),
            pltpu.VMEM((cols_n, rows_n + 1, TILE, TILE), BF),
            pltpu.VMEM((cols_n, rows_n + 1, TILE, TILE), BF),
            pltpu.VMEM((SPAN, SPAN), BF),
            pltpu.VMEM((SPAN, SPAN), BF),
            pltpu.VMEM((SPAN, SPAN), BF),
            pltpu.VMEM((MAXT, TILE, TILE), BF),
            pltpu.VMEM((groups, wide, TILE), BF),
            pltpu.VMEM((cols_n, gpr, wide, TILE), BF),
            pltpu.VMEM((wide, TPC * TILE), BF),
            pltpu.VMEM((groups, wide, TPC * TILE), BF),
            pltpu.VMEM((cols_n, gpr, wide, TPC * TILE), BF),
            pltpu.VMEM((groups, wide, TPC * TILE), BF),
            pltpu.VMEM((wide, TPC * TILE), F32),
            *[dma((rows_n,))] * 4,
            dma((rows_n + 1, cols_n)), dma((rows_n + 1, cols_n)),
            dma((rows_n, rows_n)), dma((rows_n, rows_n)),
            *[dma((2 * pairs_n, gpr))] * 4,
        ],
        compiler_params=pltpu.CompilerParams(
            collective_id=0, has_side_effects=True, vmem_limit_bytes=60000000),
    )(code, tile_lists, orders, pattern, shift, hamiltonian)


def solution(mesh):
    in_specs = (P("row", "col"), P(), P(), P(), P())
    out_specs = (P("row", "col"), P("row", "col"))
    return jax.shard_map(
        per_device, mesh=mesh, in_specs=in_specs, out_specs=out_specs, check_vma=False
    )
```
